256 devices in a mesh: grp: 8 (over x, core), dev: 32 (over y, z).
Axes of the slice: x: 4, y: 4, z: 8, core: 2. Of those that a mesh axis runs over, the one named last changes fastest.
Arguments:
- residual: bfloat16 [256, 524288], P('dev', 'grp'), may hold values from -6 to 6
- coefficients: bfloat16 [256, 128], replicated, may hold values from -0.375 to 0.375
- slot_ray: int32 [8, 32, 8, 16], P('grp', 'dev'), may hold values from 0 to 15
- slot_vox: int32 [8, 32, 8, 16], P('grp', 'dev'), may hold values from 0 to 511, as said below
- slot_count: int32 [8, 32, 8], P('grp', 'dev'), may hold values from 8 to 16, as said below
- footprint: bfloat16 [8, 32, 8, 16, 128, 128], P('grp', 'dev'), may hold values from -0.5 to 0.5
Outputs:
- basis_grad: float32 [524288, 128], P(('grp', 'dev'))
The draws below stay inside these ranges and needn't reach their ends.
Inputs may be any that keep to these rules, and one draw needn't show every extreme that they name: For each dev index d and destination group h, the 128 slots slot_vox[:, d, h, :] (used or not) name blocks of any one device of group h (blocks j * 16 to j * 16 + 15) at most 4 times. `slot_count`: every device has a list to some group with all 16 slots used.
All inputs are finite; a program needn't handle non-finite values.
Results may differ from the reference program's by a relative error of at most 0.0041.
Values may be sent and summed in bfloat16 or wider, within the bound.
No kernel may reach another device: no remote copies, remote signals or barrier semaphores. Data moves between devices by JAX's collectives and lax.ppermute only.
A program may use at most 128 MiB of HBM per device.

```python
import jax
import jax.numpy as jnp
from jax import lax

R = 128
BLK = 128
RB_DEV = 16
VB_DEV = 16
CAP = 16
F = 256
RAYS = 524288
N_GRP = 8
N_DEV = 32


def draw_slot_vox(key, part):
    pair_keys = jax.random.split(jax.random.fold_in(key, 11), N_DEV * N_GRP)
    orders = jax.vmap(lambda one_key: jax.random.permutation(one_key, N_DEV))(pair_keys).reshape(N_DEV, N_GRP, N_DEV)
    source = jnp.arange(N_GRP)[:, None]
    place = jnp.arange(CAP)[None, :]
    bucket = (place * N_GRP + source) // (N_GRP * CAP // N_DEV)
    owner = orders[:, :, bucket]
    owner = jnp.transpose(owner, (2, 0, 1, 3))
    inner = jax.random.randint(jax.random.fold_in(key, 12), owner.shape, 0, VB_DEV)
    return (owner * VB_DEV + inner).astype(jnp.int32)


def draw_slot_count(key, part):
    counts = jax.random.randint(jax.random.fold_in(key, 21), (N_GRP, N_DEV, N_GRP), CAP // 2, CAP + 1)
    full_at = jax.random.randint(jax.random.fold_in(key, 22), (N_GRP, N_DEV, 1), 0, N_GRP)
    counts = jnp.where(jnp.arange(N_GRP)[None, None, :] == full_at, CAP, counts)
    return counts.astype(jnp.int32)


def place_ends(drawn, stream_key, smallest, high):
    longest = drawn.shape.index(max(drawn.shape))
    spots = []
    for shift in (0, 1):
        where = [jax.random.randint(jax.random.fold_in(stream_key, axis), (), 0, length) for axis, length in enumerate(drawn.shape)]
        where[longest] = (where[longest] + shift) % drawn.shape[longest]
        spots.append(tuple(where))
    return drawn.at[spots[0]].set(smallest).at[spots[1]].set(high)


def levels(key, extent, cuts, least, top_value):
    loudness, own = 1.0, jax.random.fold_in(key, 6)
    for position, shards_of in cuts:
        steps = jnp.exp(jax.random.uniform(jax.random.fold_in(own, position), (shards_of,), jnp.float32, least / len(cuts), top_value / len(cuts)))
        loudness = loudness * jnp.repeat(steps, extent[position] // shards_of).reshape([-1 if axis == position else 1 for axis in range(len(extent))])
    return loudness


def normal_values(rng, shape, scale, limit, cuts=(), kind=jnp.bfloat16):
    values = scale * jax.random.normal(rng, shape, jnp.float32)
    if cuts:
        values = values * levels(rng, shape, cuts, -0.22, 0.18)
    return jnp.clip(values, -limit, limit).astype(kind)


def setup_inputs(seed: int = 0) -> dict:
    streams_of = jax.random.split(jax.random.key(seed), 7)
    return {
        "residual": normal_values(streams_of[0], (F, RAYS), 1.0, 6.0, ((0, 32), (1, 8))),
        "coefficients": normal_values(streams_of[1], (F, R), F ** -0.5, 0.375),
        "slot_ray": place_ends(jax.random.randint(streams_of[2], (N_GRP, N_DEV, N_GRP, CAP), 0, RB_DEV), jax.random.fold_in(streams_of[2], 1), 0, RB_DEV - 1).astype(jnp.int32),
        "slot_vox": draw_slot_vox(jax.random.fold_in(streams_of[6], 71), 0),
        "slot_count": draw_slot_count(jax.random.fold_in(streams_of[6], 71), 0),
        "footprint": normal_values(streams_of[5], (N_GRP, N_DEV, N_GRP, CAP, BLK, BLK), BLK ** -0.5, 0.5, ((0, 8), (1, 32))),
    }


def reference(residual, coefficients, slot_ray, slot_vox, slot_count, footprint):
    projected = lax.dot_general(residual, coefficients, (((0,), (0,)), ((), ())), preferred_element_type=jnp.float32).astype(jnp.bfloat16)
    sources = N_GRP * N_DEV
    ray_blocks = projected.reshape(sources, RB_DEV, BLK, R)
    items = (ray_blocks, slot_ray.reshape(sources, N_GRP, CAP), slot_vox.reshape(sources, N_GRP, CAP), slot_count.reshape(sources, N_GRP), footprint.reshape(sources, N_GRP, CAP, BLK, BLK))

    def add_source(total, item):
        blocks, rays, voxels, counts, weights = item
        chosen = blocks[rays].astype(jnp.float32)
        adjoint = jnp.einsum("gsij,gsik->gsjk", weights.astype(jnp.float32), chosen)
        used = jnp.arange(CAP)[None, :] < counts[:, None]
        adjoint = jnp.where(used[:, :, None, None], adjoint, jnp.zeros_like(adjoint)).astype(jnp.bfloat16)
        adjoint = lax.optimization_barrier(adjoint).astype(total.dtype)
        total = total.at[jnp.arange(N_GRP)[:, None], voxels].add(adjoint)
        return total, None

    total = jnp.zeros((N_GRP, VB_DEV * N_DEV, BLK, R), jnp.float32)
    total, _ = lax.scan(add_source, total, items)
    return total.reshape(N_GRP * VB_DEV * N_DEV * BLK, R)
```

```python
import functools

import jax
import jax.numpy as jnp
from jax import lax
from jax.experimental import pallas as pl
from jax.experimental.pallas import tpu as pltpu
from jax.sharding import PartitionSpec as P

BLK = 128
CAP = 16
CORES = 2
NX = 4
NY = 4
NZ = 8
VB = 16
PART = CORES * CAP
CHUNKS = (48, 48, 32)


def adjoint_kernel(rows, rays_ref, place_ref, own_ref, par_ref, fpo_ref, fpr_ref, *rest):
    nouts = NX * len(rows)
    outs, buf, sems = rest[:nouts], rest[nouts], rest[nouts + 1]
    x, c = place_ref[0], place_ref[1]
    low = rows[0][0]
    high = rows[-1][1]
    copies = []
    for k in range(NX):
        to = lax.rem(x + k, NX)
        copies.append(pltpu.make_async_copy(fpo_ref.at[to * CORES + c], buf.at[k, 0], sems.at[k, 0]))
        copies.append(pltpu.make_async_copy(fpr_ref.at[to], buf.at[k, 1], sems.at[k, 1]))
    for copy in copies:
        copy.start()
    for k in range(NX):
        for side, proj in enumerate((own_ref, par_ref)):
            copies[k * 2 + side].wait()

            def slots(i, carry, k=k, side=side, proj=proj):
                for u in range(8):
                    s = i * 8 + u
                    ray = rays_ref[(k * 2 + side) * CAP + s]
                    col = pl.multiple_of(jnp.maximum(ray, 0) * BLK, BLK)
                    block = jnp.dot(
                        proj[low:high, pl.ds(col, BLK)], buf[k, side, s], preferred_element_type=jnp.float32
                    )
                    block = jnp.where(ray >= 0, block, 0.0).astype(jnp.bfloat16)
                    for j, (lo, hi) in enumerate(rows):
                        outs[j * NX + k][side * CAP + s] = block[lo - low : hi - low]
                return carry

            lax.fori_loop(0, CAP // 8, slots, 0)


def adjoints(rows, rays, place, own, par, fpo, fpr):
    vmem = pl.BlockSpec(memory_space=pltpu.VMEM)
    smem = pl.BlockSpec(memory_space=pltpu.SMEM)
    hbm = pl.BlockSpec(memory_space=pl.ANY)
    shapes = [
        jax.ShapeDtypeStruct((PART, hi - lo, BLK), jnp.bfloat16) for lo, hi in rows for _ in range(NX)
    ]
    return pl.pallas_call(
        functools.partial(adjoint_kernel, rows),
        out_shape=shapes,
        in_specs=[smem, smem, vmem, vmem, hbm, hbm],
        out_specs=[vmem] * len(shapes),
        scratch_shapes=[
            pltpu.VMEM((NX, CORES, CAP, BLK, BLK), jnp.bfloat16),
            pltpu.SemaphoreType.DMA((NX, CORES)),
        ],
        cost_estimate=pl.CostEstimate(flops=2 * 128**4, bytes_accessed=6 << 20, transcendentals=0),
        name="adjoint",
    )(rays, place, own, par, fpo, fpr)


def pack_kernel(src_ref, *refs):
    ins, outs, buf, sems = refs[:NX], refs[NX : NX + NY], refs[NX + NY], refs[NX + NY + 1]
    copies = [
        pltpu.make_async_copy(ins[k], buf.at[pl.ds(k * PART, PART)], sems.at[k]) for k in range(NX)
    ]
    for copy in copies:
        copy.start()
    for copy in copies:
        copy.wait()
    for k in range(NY):

        def move(i, carry, k=k):
            for u in range(8):
                p = i * 8 + u
                outs[k][p] = buf[src_ref[k * PART + p]]
            return carry

        lax.fori_loop(0, PART // 8, move, 0)


def pack(src, parts):
    vmem = pl.BlockSpec(memory_space=pltpu.VMEM)
    smem = pl.BlockSpec(memory_space=pltpu.SMEM)
    hbm = pl.BlockSpec(memory_space=pl.ANY)
    shape = parts[0].shape
    return pl.pallas_call(
        pack_kernel,
        out_shape=[jax.ShapeDtypeStruct(shape, jnp.bfloat16)] * NY,
        in_specs=[smem] + [hbm] * NX,
        out_specs=[vmem] * NY,
        scratch_shapes=[
            pltpu.VMEM((NX * PART,) + shape[1:], jnp.bfloat16),
            pltpu.SemaphoreType.DMA((NX,)),
        ],
        cost_estimate=pl.CostEstimate(flops=0, bytes_accessed=4 << 20, transcendentals=0),
        name="pack",
    )(src, *parts)


def gather_kernel(up_far, at_ref, *refs):
    ins, dense, up, down = refs[:NY], refs[NY], refs[NY + 1], refs[NY + 2]
    dense[...] = jnp.zeros_like(dense)
    for k in range(NY):

        def add(i, carry, k=k):
            for u in range(8):
                p = i * 8 + u
                at = at_ref[k * PART + p]
                dense[at] = dense[at] + ins[k][p].astype(jnp.float32)
            return carry

        lax.fori_loop(0, PART // 8, add, 0)
    up[...] = dense[up_far * VB : (up_far + 1) * VB].astype(jnp.bfloat16)
    first = up_far + 1
    down[...] = dense[first * VB : (first + 1) * VB].astype(jnp.bfloat16)


def gather(up_far, at, parts):
    vmem = pl.BlockSpec(memory_space=pltpu.VMEM)
    smem = pl.BlockSpec(memory_space=pltpu.SMEM)
    rows = parts[0].shape[1]
    send = jax.ShapeDtypeStruct((VB, rows, BLK), jnp.bfloat16)
    return pl.pallas_call(
        functools.partial(gather_kernel, up_far),
        out_shape=[jax.ShapeDtypeStruct((NZ * VB, rows, BLK), jnp.float32), send, send],
        in_specs=[smem] + [vmem] * NY,
        out_specs=[vmem] * 3,
        cost_estimate=pl.CostEstimate(flops=0, bytes_accessed=4 << 20, transcendentals=0),
        name="gather",
    )(at, *parts)


def finish_kernel(*refs):
    parts, out = refs[:-1], refs[-1]
    for b in range(VB):
        rows = jnp.concatenate([part[b] for part in parts], axis=0)
        out[b * BLK : (b + 1) * BLK, :] = rows.T


def finish(parts):
    vmem = pl.BlockSpec(memory_space=pltpu.VMEM)
    return pl.pallas_call(
        finish_kernel,
        out_shape=jax.ShapeDtypeStruct((VB * BLK, BLK), jnp.float32),
        in_specs=[vmem] * len(parts),
        out_specs=vmem,
        cost_estimate=pl.CostEstimate(flops=0, bytes_accessed=2 << 20, transcendentals=0),
        name="finish",
    )(*parts)


def x_shift(k):
    return [(x * CORES + c, (x + k) % NX * CORES + c) for x in range(NX) for c in range(CORES)]


def core_swap():
    return [(g, g ^ 1) for g in range(NX * CORES)]


def y_shift(k):
    return [(y * NZ + z, (y + k) % NY * NZ + z) for y in range(NY) for z in range(NZ)]


def z_shift(k):
    return [(y * NZ + z, y * NZ + (z + k) % NZ) for y in range(NY) for z in range(NZ)]


def exchange(parts, axis, shift):
    return [parts[0]] + [lax.ppermute(parts[k], axis, shift(k)) for k in range(1, len(parts))]


def routes(slot_ray, slot_vox, slot_count, x, c, y, z):
    used = jnp.arange(CAP, dtype=jnp.int32)[None, :] < slot_count[:, None]
    lists = jnp.concatenate([jnp.where(used, slot_ray, -1), slot_vox], axis=1).reshape(NX, CORES, 2 * CAP)
    own = lax.dynamic_index_in_dim(lists, c, 1, keepdims=False)
    par = lax.ppermute(lax.dynamic_index_in_dim(lists, 1 - c, 1, keepdims=False), "grp", core_swap())
    both = jnp.stack([own, par], axis=1)
    both = lax.dynamic_slice_in_dim(jnp.concatenate([both, both], axis=0), x, NX, 0)
    rays = both[:, :, :CAP].reshape(NX * PART)
    vox = both[:, :, CAP:].reshape(NX, PART)
    vox = jnp.concatenate(exchange([vox[k] for k in range(NX)], "grp", x_shift))
    key = lax.rem(vox // (NZ * VB) - y + NY, NY)
    slots = jnp.arange(NX * PART, dtype=jnp.int32)
    same = (key[:, None] == key[None, :]) & (slots[None, :] < slots[:, None])
    target = key * PART + jnp.sum(same.astype(jnp.int32), axis=1)
    hit = (target[None, :] == slots[:, None]).astype(jnp.int32)
    src = jnp.sum(hit * slots[None, :], axis=1)
    place = lax.rem(lax.rem(vox // VB, NZ) - z + NZ, NZ) * VB + lax.rem(vox, VB)
    at = jnp.sum(hit * place[None, :], axis=1).reshape(NY, PART)
    at = jnp.concatenate(exchange([at[k] for k in range(NY)], "dev", y_shift))
    return rays, src, at


def ring(up_far, dense, up, down):
    delta = up_far
    for d in range(up_far, 0, -1):
        up = lax.ppermute(up, "dev", z_shift(1))
        if d > 1:
            up = (up.astype(jnp.float32) + dense[(d - 1) * VB : d * VB]).astype(jnp.bfloat16)
    for d in range(up_far + 1, NZ):
        down = lax.ppermute(down, "dev", z_shift(NZ - 1))
        if d < NZ - 1:
            down = (down.astype(jnp.float32) + dense[(d + 1) * VB : (d + 2) * VB]).astype(jnp.bfloat16)
    return dense[:VB] + up.astype(jnp.float32) + down.astype(jnp.float32)


def body(residual, coefficients, slot_ray, slot_vox, slot_count, footprint):
    g, d = lax.axis_index("grp"), lax.axis_index("dev")
    x, c, y, z = g // CORES, g % CORES, d // NZ, d % NZ
    tiles = footprint[0, 0]
    panel = lax.all_to_all(residual, "dev", split_axis=1, concat_axis=0, tiled=True)
    rays, src, at = routes(slot_ray[0, 0], slot_vox[0, 0], slot_count[0, 0], x, c, y, z)
    place = jnp.stack([x, c]).astype(jnp.int32)
    send = lax.dynamic_index_in_dim(tiles.reshape((NX, CORES) + tiles.shape[1:]), 1 - c, 1, keepdims=False)
    got = lax.ppermute(send, "grp", core_swap())
    own = lax.dot_general(
        coefficients, panel, (((0,), (0,)), ((), ())), preferred_element_type=jnp.float32
    ).astype(jnp.bfloat16)
    par = lax.ppermute(own, "grp", core_swap())
    rows, low = [], 0
    for size in CHUNKS:
        rows.append((low, low + size))
        low += size
    first = adjoints(tuple(rows[:1]), rays, place, own, par, tiles, got)
    later = adjoints(tuple(rows[1:]), rays, place, own, par, tiles, got)
    made = list(first) + list(later)
    sums = []
    for i in range(len(rows)):
        parts = exchange(made[i * NX : (i + 1) * NX], "grp", x_shift)
        parts = exchange(pack(src, parts), "dev", y_shift)
        up_far = NZ // 2 - i % 2
        sums.append(ring(up_far, *gather(up_far, at, parts)))
    return finish(sums)


def solution(mesh):
    placed = (
        P("dev", "grp"),
        P(),
        P("grp", "dev", None, None),
        P("grp", "dev", None, None),
        P("grp", "dev", None),
        P("grp", "dev", None, None, None, None),
    )
    return jax.shard_map(
        body, mesh=mesh, in_specs=placed, out_specs=P(("grp", "dev"), None), check_vma=False
    )
```

```python
import functools

import jax
import jax.numpy as jnp
from jax import lax
from jax.experimental import pallas as pl
from jax.experimental.pallas import tpu as pltpu
from jax.sharding import PartitionSpec as P


BLK = 128
CAP = 16
CORES = 2
NX = 4
NY = 4
NZ = 8
VB = 16
PART = CORES * CAP
CHUNKS = (48, 48, 32)
HOPS = NZ // 2
VMEM_LIMIT = 10 << 20


VMEM = pl.BlockSpec(memory_space=pltpu.VMEM)
SMEM = pl.BlockSpec(memory_space=pltpu.SMEM)


def call(kernel, out_shape, ins, smems, flops=0, scratch=()):
    specs = [SMEM] * smems + [VMEM] * (len(ins) - smems)
    many = isinstance(out_shape, list)
    return pl.pallas_call(
        kernel,
        out_shape=out_shape,
        in_specs=specs,
        out_specs=[VMEM] * len(out_shape) if many else VMEM,
        scratch_shapes=list(scratch),
        compiler_params=pltpu.CompilerParams(vmem_limit_bytes=VMEM_LIMIT),
        cost_estimate=pl.CostEstimate(flops=flops, bytes_accessed=4 << 20, transcendentals=0),
    )(*ins)


def adjoint_kernel(low, high, rays_ref, place_ref, own_ref, par_ref, fpo_ref, fpr_ref, *outs):
    rows = high - low
    blank = jnp.zeros((rows, BLK), jnp.bfloat16)
    for k in range(NX):
        to = lax.rem(place_ref[0] + k, NX)
        for side, (proj, tiles) in enumerate(((own_ref, fpo_ref), (par_ref, fpr_ref))):

            def pairs(i, carry, k=k, side=side, proj=proj, tiles=tiles, to=to):
                for u in range(4):
                    pair = i * 4 + u
                    ray = [rays_ref[(k * CORES + side) * CAP + pair * 2 + v] for v in range(2)]
                    cols = [pl.multiple_of(jnp.maximum(r, 0) * BLK, BLK) for r in ray]
                    left, right = [proj[low:high, pl.ds(col, BLK)] for col in cols]
                    left = jnp.where(ray[0] >= 0, left, blank)
                    right = jnp.where(ray[1] >= 0, right, blank)
                    both = jnp.concatenate(
                        [jnp.concatenate([left, blank], axis=1), jnp.concatenate([blank, right], axis=1)], axis=0
                    )
                    made = jnp.dot(both, tiles[to, pair], preferred_element_type=jnp.float32).astype(jnp.bfloat16)
                    outs[k][side * CAP + pair * 2] = made[:rows]
                    outs[k][side * CAP + pair * 2 + 1] = made[rows:]
                return carry

            lax.fori_loop(0, CAP // 8, pairs, 0)


def pack_kernel(src_ref, *refs):
    ins, outs, buf = refs[:NX], refs[NX : NX + NY], refs[NX + NY]
    for k in range(NX):
        buf[k * PART : (k + 1) * PART] = ins[k][...]
    for k in range(NY):

        def move(i, carry, k=k):
            for u in range(8):
                p = i * 8 + u
                outs[k][p] = buf[src_ref[k * PART + p]]
            return carry

        lax.fori_loop(0, PART // 8, move, 0)


def gather_kernel(up_far, at_ref, *refs):
    ins, dense, up, down = refs[:NY], refs[NY], refs[NY + 1], refs[NY + 2]
    dense[...] = jnp.zeros_like(dense)
    for k in range(NY):

        def add(i, carry, k=k):
            for u in range(8):
                p = i * 8 + u
                at = at_ref[k * PART + p]
                dense[at] = dense[at] + ins[k][p].astype(jnp.float32)
            return carry

        lax.fori_loop(0, PART // 8, add, 0)
    up[...] = dense[up_far * VB : (up_far + 1) * VB].astype(jnp.bfloat16)
    down[...] = dense[(up_far + 1) * VB : (up_far + 2) * VB].astype(jnp.bfloat16)


def hop_kernel(places, dense, *refs):
    n = len(places)
    for came, goes, at in zip(refs[:n], refs[n:], places):
        goes[...] = (came[...].astype(jnp.float32) + dense[at * VB : (at + 1) * VB]).astype(jnp.bfloat16)


def finish_kernel(*refs):
    parts, out = refs[:-1], refs[-1]
    for b in range(VB):
        rows = [
            parts[i][b] + parts[i + 1][b].astype(jnp.float32) + parts[i + 2][b].astype(jnp.float32)
            for i in range(0, len(parts), 3)
        ]
        out[b * BLK : (b + 1) * BLK, :] = jnp.concatenate(rows, axis=0).T


def x_shift(k):
    return [(x * CORES + c, (x + k) % NX * CORES + c) for x in range(NX) for c in range(CORES)]


def core_swap():
    return [(g, g ^ 1) for g in range(NX * CORES)]


def y_shift(k):
    return [(y * NZ + z, (y + k) % NY * NZ + z) for y in range(NY) for z in range(NZ)]


def z_shift(k):
    return [(y * NZ + z, y * NZ + (z + k) % NZ) for y in range(NY) for z in range(NZ)]


def exchange(parts, axis, shift):
    moved = [parts[0]]
    for k in range(1, len(parts)):
        moved.append(lax.ppermute(parts[k], axis, shift(k)))
    return moved


def routes(slot_ray, slot_vox, slot_count, x, c, y, z):
    used = jnp.arange(CAP, dtype=jnp.int32)[None, :] < slot_count[:, None]
    lists = jnp.concatenate([jnp.where(used, slot_ray, -1), slot_vox], axis=1).reshape(NX, CORES, 2 * CAP)
    own = lax.dynamic_index_in_dim(lists, c, 1, keepdims=False)
    par = lax.ppermute(lax.dynamic_index_in_dim(lists, 1 - c, 1, keepdims=False), "grp", core_swap())
    both = jnp.stack([own, par], axis=1)
    both = lax.dynamic_slice_in_dim(jnp.concatenate([both, both], axis=0), x, NX, 0)
    rays = both[:, :, :CAP].reshape(NX * PART)
    vox = both[:, :, CAP:].reshape(NX, PART)
    vox = jnp.concatenate(exchange([vox[k] for k in range(NX)], "grp", x_shift))
    key = lax.rem(vox // (NZ * VB) - y + NY, NY)
    slots = jnp.arange(NX * PART, dtype=jnp.int32)
    same = (key[:, None] == key[None, :]) & (slots[None, :] < slots[:, None])
    target = key * PART + jnp.sum(same.astype(jnp.int32), axis=1)
    hit = (target[None, :] == slots[:, None]).astype(jnp.int32)
    src = jnp.sum(hit * slots[None, :], axis=1)
    place = lax.rem(lax.rem(vox // VB, NZ) - z + NZ, NZ) * VB + lax.rem(vox, VB)
    at = jnp.sum(hit * place[None, :], axis=1).reshape(NY, PART)
    at = jnp.concatenate(exchange([at[k] for k in range(NY)], "dev", y_shift))
    return rays, src, at


def turns(i):
    up_far = HOPS - i % 2
    return list(range(up_far, 0, -1)), list(range(up_far + 1, NZ))


def ring(i, dense, up, down):
    ups, downs = turns(i)
    for hop in range(HOPS):
        sent = []
        for part, far, step in ((up, ups, 1), (down, downs, NZ - 1)):
            if hop < len(far):
                part = lax.ppermute(part, "dev", z_shift(step))
            sent.append(part)
        up, down = sent
        places = [far[hop + 1] for far in (ups, downs) if hop + 1 < len(far)]
        if places:
            going = [part for part, far in ((up, ups), (down, downs)) if hop + 1 < len(far)]
            going = call(
                functools.partial(hop_kernel, places),
                [pltpu.VMEM(part.shape, part.dtype) for part in going],
                [dense] + going,
                0,
            )
            up = going[0] if hop + 1 < len(ups) else up
            down = going[-1] if hop + 1 < len(downs) else down
    return [dense, up, down]


def body(residual, coefficients, slot_ray, slot_vox, slot_count, footprint):
    g, d = lax.axis_index("grp"), lax.axis_index("dev")
    x, c, y, z = g // CORES, g % CORES, d // NZ, d % NZ
    panel = lax.all_to_all(residual, "dev", split_axis=1, concat_axis=0, tiled=True)
    tables = routes(slot_ray[0, 0], slot_vox[0, 0], slot_count[0, 0], x, c, y, z)
    place = jnp.stack([x, c]).astype(jnp.int32)
    tiles = footprint.reshape(NX, CORES, CAP // 2, 2 * BLK, BLK)
    fpo = lax.dynamic_index_in_dim(tiles, c, 1, keepdims=False)
    fpr = lax.dynamic_index_in_dim(tiles, 1 - c, 1, keepdims=False)
    fpr = lax.ppermute(fpr, "grp", core_swap())
    panel, (rays, src, at), place, fpo, fpr = lax.optimization_barrier((panel, tables, place, fpo, fpr))
    own = lax.dot_general(
        coefficients, panel, (((0,), (0,)), ((), ())), preferred_element_type=jnp.float32
    ).astype(jnp.bfloat16)
    par = lax.ppermute(own, "grp", core_swap())
    ends, low = [], 0
    for i, size in enumerate(CHUNKS):
        block = pltpu.VMEM((PART, size, BLK), jnp.bfloat16)
        parts = call(
            functools.partial(adjoint_kernel, low, low + size), [block] * NX, [rays, place, own, par, fpo, fpr], 2
        )
        low += size
        parts = exchange(parts, "grp", x_shift)
        parts = call(
            pack_kernel, [block] * NY, [src] + parts, 1, scratch=[pltpu.VMEM((NX * PART, size, BLK), jnp.bfloat16)]
        )
        parts = exchange(parts, "dev", y_shift)
        send = pltpu.VMEM((VB, size, BLK), jnp.bfloat16)
        dense, up, down = call(
            functools.partial(gather_kernel, turns(i)[0][0]),
            [pltpu.VMEM((NZ * VB, size, BLK), jnp.float32), send, send],
            [at] + parts,
            1,
        )
        ends += ring(i, dense, up, down)
    return call(finish_kernel, jax.ShapeDtypeStruct((VB * BLK, BLK), jnp.float32), ends, 0)


def solution(mesh):
    placed = (
        P("dev", "grp"),
        P(),
        P("grp", "dev", None, None),
        P("grp", "dev", None, None),
        P("grp", "dev", None),
        P("grp", "dev", None, None, None, None),
    )

    return jax.shard_map(body, mesh=mesh, in_specs=placed, out_specs=P(("grp", "dev"), None), check_vma=False)
```

```python
import functools

import jax
import jax.numpy as jnp
from jax import lax
from jax.experimental import pallas as pl
from jax.experimental.pallas import tpu as pltpu
from jax.sharding import PartitionSpec as P


BLK = 128
CAP = 16
CORES = 2
NX = 4
NY = 4
NZ = 8
VB = 16
PART = CORES * CAP
CHUNKS = (32, 48, 48)
HOPS = NZ // 2
VMEM_LIMIT = 10 << 20
RINGS = ((0, 1), (2,))


VMEM = pl.BlockSpec(memory_space=pltpu.VMEM)
SMEM = pl.BlockSpec(memory_space=pltpu.SMEM)


def call(kernel, out_shape, ins, smems, flops=0, scratch=()):
    specs = [SMEM] * smems + [VMEM] * (len(ins) - smems)
    many = isinstance(out_shape, list)
    return pl.pallas_call(
        kernel,
        out_shape=out_shape,
        in_specs=specs,
        out_specs=[VMEM] * len(out_shape) if many else VMEM,
        scratch_shapes=list(scratch),
        compiler_params=pltpu.CompilerParams(vmem_limit_bytes=VMEM_LIMIT),
        cost_estimate=pl.CostEstimate(flops=flops, bytes_accessed=4 << 20, transcendentals=0),
    )(*ins)


def adjoint_kernel(rows, rays_ref, place_ref, own_ref, par_ref, fpo_ref, fpr_ref, *outs):
    low, high = rows[0][0], rows[-1][1]
    size = high - low
    blank = jnp.zeros((size, BLK), jnp.bfloat16)
    for k in range(NX):
        to = lax.rem(place_ref[0] + k, NX)
        for side, (proj, tiles) in enumerate(((own_ref, fpo_ref), (par_ref, fpr_ref))):

            for quad in range(CAP // 4):
                first = (k * CORES + side) * CAP + quad * 4
                stack = []
                for v in range(4):
                    ray = rays_ref[first + v]
                    rank = proj[low:high, pl.ds(pl.multiple_of(jnp.maximum(ray, 0) * BLK, BLK), BLK)]
                    rank = jnp.where(ray >= 0, rank, blank)
                    stack.append(jnp.concatenate([blank, rank] if v % 2 else [rank, blank], axis=1))
                made = jnp.dot(
                    jnp.concatenate(stack, axis=0),
                    jnp.concatenate([tiles[to, quad * 2], tiles[to, quad * 2 + 1]], axis=1),
                    preferred_element_type=jnp.float32,
                )
                for v in range(4):
                    block = made[v * size : (v + 1) * size, (v // 2) * BLK : (v // 2 + 1) * BLK].astype(jnp.bfloat16)
                    for j, (lo, hi) in enumerate(rows):
                        outs[j * NX + k][side * CAP + quad * 4 + v] = block[lo - low : hi - low]


def pack_kernel(src_ref, *refs):
    ins, outs, buf = refs[:NX], refs[NX : NX + NY], refs[NX + NY]
    for k in range(NX):
        buf[k * PART : (k + 1) * PART] = ins[k][...]
    for k in range(NY):

        def move(i, carry, k=k):
            for u in range(8):
                p = i * 8 + u
                outs[k][p] = buf[src_ref[k * PART + p]]
            return carry

        lax.fori_loop(0, PART // 8, move, 0)


def gather_kernel(up_far, earlier, at_ref, *refs):
    ins, before, dense = refs[:NY], refs[NY : NY + earlier], refs[NY + earlier]
    sends = refs[NY + earlier + 1 :]
    dense[...] = jnp.zeros_like(dense)
    for k in range(NY):

        def add(i, carry, k=k):
            for u in range(4):
                p = i * 4 + u
                at = at_ref[k * PART + p]
                dense[at] = dense[at] + ins[k][p].astype(jnp.float32)
            return carry

        lax.fori_loop(0, PART // 4, add, 0)
    for send, far in zip(sends, (up_far, up_far + 1)):
        low = 0
        for part in tuple(before) + (dense,):
            high = low + part.shape[1]
            send[:, low:high, :] = part[far * VB : (far + 1) * VB].astype(jnp.bfloat16)
            low = high


def hop_kernel(places, count, *refs):
    dense, refs = refs[:count], refs[count:]
    n = len(places)
    for came, goes, at in zip(refs[:n], refs[n:], places):
        low = 0
        for part in dense:
            high = low + part.shape[1]
            mine = part[at * VB : (at + 1) * VB]
            goes[:, low:high, :] = (came[:, low:high, :].astype(jnp.float32) + mine).astype(jnp.bfloat16)
            low = high


def finish_kernel(groups, *refs):
    parts, out = refs[:-1], refs[-1]
    for b in range(VB):
        rows, at = [], 0
        for group in groups:
            up, down = parts[at + len(group)], parts[at + len(group) + 1]
            low = 0
            for part in parts[at : at + len(group)]:
                high = low + part.shape[1]
                rows.append(
                    part[b] + up[b, low:high, :].astype(jnp.float32) + down[b, low:high, :].astype(jnp.float32)
                )
                low = high
            at += len(group) + 2
        out[b * BLK : (b + 1) * BLK, :] = jnp.concatenate(rows, axis=0).T


def x_shift(k):
    return [(x * CORES + c, (x + k) % NX * CORES + c) for x in range(NX) for c in range(CORES)]


def core_swap():
    return [(g, g ^ 1) for g in range(NX * CORES)]


def y_shift(k):
    return [(y * NZ + z, (y + k) % NY * NZ + z) for y in range(NY) for z in range(NZ)]


def z_shift(k):
    return [(y * NZ + z, y * NZ + (z + k) % NZ) for y in range(NY) for z in range(NZ)]


def exchange(parts, axis, shift):
    moved = [parts[0]]
    for k in range(1, len(parts)):
        moved.append(lax.ppermute(parts[k], axis, shift(k)))
    return moved


def spread(known, axis, near):
    for pairs in near:
        known = jnp.concatenate([known, lax.ppermute(known, axis, pairs)], axis=0)
    return known


def flip(size, unit, bit):
    return [(i, i ^ (bit * unit)) for i in range(size)]


def routes(slot_ray, slot_vox, slot_count, x, c, y, z):
    used = jnp.arange(CAP, dtype=jnp.int32)[None, :] < slot_count[:, None]
    lists = jnp.concatenate([jnp.where(used, slot_ray, -1), slot_vox], axis=1)
    size = NX * CORES
    near = [flip(size, 1, 1), flip(size, CORES, 1), flip(size, CORES, 2)]
    table = spread(lists[None], "grp", near)
    table = table.reshape(NX, CORES, NX, CORES, 2 * CAP)
    mine = lax.dynamic_index_in_dim(table, c, 3, keepdims=False)
    rays = lax.dynamic_slice_in_dim(jnp.concatenate([mine[0]] * 2, axis=1), x, NX, 1)
    rays = jnp.transpose(rays, (1, 0, 2))[:, :, :CAP].reshape(NX * PART)
    vox = lax.dynamic_index_in_dim(mine, x, 2, keepdims=False)[:, :, CAP:].reshape(NX, PART)
    entry = jnp.bitwise_xor(x, lax.rem(x - jnp.arange(NX, dtype=jnp.int32) + NX, NX))
    pick = (entry[:, None] == jnp.arange(NX, dtype=jnp.int32)[None, :]).astype(jnp.int32)
    vox = jnp.sum(pick[:, :, None] * vox[None], axis=1).reshape(1, NX * PART)
    near = [flip(NY * NZ, NZ, 1), flip(NY * NZ, NZ, 2)]
    vox = spread(vox, "dev", near)
    key = lax.rem(vox // (NZ * VB), NY)
    there = jnp.bitwise_xor(y, jnp.arange(NY, dtype=jnp.int32))
    turn = lax.rem(key - there[:, None] + NY, NY)
    slots = jnp.arange(NX * PART, dtype=jnp.int32)
    same = (turn[:, :, None] == turn[:, None, :]) & (slots[None, None, :] < slots[None, :, None])
    target = turn * PART + jnp.sum(same.astype(jnp.int32), axis=2)
    hit = (target[:, None, :] == slots[None, :, None]).astype(jnp.int32)
    src = jnp.sum(hit[0] * slots[None, :], axis=1)
    place = lax.rem(lax.rem(vox // VB, NZ) - z + NZ, NZ) * VB + lax.rem(vox, VB)
    at = jnp.sum(hit * place[:, None, :], axis=2).reshape(NY, NY, PART)
    entry = jnp.bitwise_xor(y, lax.rem(y - jnp.arange(NY, dtype=jnp.int32) + NY, NY))
    pick = (entry[:, None] == jnp.arange(NY, dtype=jnp.int32)[None, :]).astype(jnp.int32)
    at = jnp.sum(pick[:, :, None] * jnp.transpose(at, (1, 0, 2)), axis=1).reshape(NY * PART)
    return rays, src, at


def turns(r):
    up_far = HOPS - r % 2
    return list(range(up_far, 0, -1)), list(range(up_far + 1, NZ))


def ring(r, dense, up, down):
    ups, downs = turns(r)
    for hop in range(HOPS):
        sent = []
        for part, far, step in ((up, ups, 1), (down, downs, NZ - 1)):
            if hop < len(far):
                part = lax.ppermute(part, "dev", z_shift(step))
            sent.append(part)
        up, down = sent
        places = [far[hop + 1] for far in (ups, downs) if hop + 1 < len(far)]
        if places:
            going = [part for part, far in ((up, ups), (down, downs)) if hop + 1 < len(far)]
            going = call(
                functools.partial(hop_kernel, places, len(dense)),
                [pltpu.VMEM(part.shape, part.dtype) for part in going],
                dense + going,
                0,
            )
            up = going[0] if hop + 1 < len(ups) else up
            down = going[-1] if hop + 1 < len(downs) else down
    return dense + [up, down]


def body(residual, coefficients, slot_ray, slot_vox, slot_count, footprint):
    g, d = lax.axis_index("grp"), lax.axis_index("dev")
    x, c, y, z = g // CORES, g % CORES, d // NZ, d % NZ
    panel = lax.all_to_all(residual, "dev", split_axis=1, concat_axis=0, tiled=True)
    tables = routes(slot_ray[0, 0], slot_vox[0, 0], slot_count[0, 0], x, c, y, z)
    place = jnp.stack([x, c]).astype(jnp.int32)
    tiles = footprint.reshape(NX, CORES, CAP // 2, 2 * BLK, BLK)
    fpo = lax.dynamic_index_in_dim(tiles, c, 1, keepdims=False)
    fpr = lax.dynamic_index_in_dim(tiles, 1 - c, 1, keepdims=False)
    fpr = lax.ppermute(fpr, "grp", core_swap())
    panel, (rays, src, at), place, fpo, fpr = lax.optimization_barrier((panel, tables, place, fpo, fpr))
    own = lax.dot_general(
        coefficients, panel, (((0,), (0,)), ((), ())), preferred_element_type=jnp.float32
    ).astype(jnp.bfloat16)
    par = lax.ppermute(own, "grp", core_swap())
    rows = [(sum(CHUNKS[:i]), sum(CHUNKS[: i + 1])) for i in range(len(CHUNKS))]
    made = []
    for some in (rows[:1], rows[1:]):
        made += call(
            functools.partial(adjoint_kernel, some),
            [pltpu.VMEM((PART, hi - lo, BLK), jnp.bfloat16) for lo, hi in some for _ in range(NX)],
            [rays, place, own, par, fpo, fpr],
            2,
        )
    ends = []
    for r, group in enumerate(RINGS):
        dense = []
        for i in group:
            size = CHUNKS[i]
            block = pltpu.VMEM((PART, size, BLK), jnp.bfloat16)
            parts = exchange(made[i * NX : (i + 1) * NX], "grp", x_shift)
            parts = call(
                pack_kernel, [block] * NY, [src] + parts, 1, scratch=[pltpu.VMEM((NX * PART, size, BLK), jnp.bfloat16)]
            )
            parts = exchange(parts, "dev", y_shift)
            sends = []
            if i == group[-1]:
                sends = [pltpu.VMEM((VB, sum(CHUNKS[j] for j in group), BLK), jnp.bfloat16)] * 2
            before = dense if sends else []
            came = call(
                functools.partial(gather_kernel, turns(r)[0][0], len(before)),
                [pltpu.VMEM((NZ * VB, size, BLK), jnp.float32)] + sends,
                [at] + parts + before,
                1,
            )
            dense = dense + [came[0]]
        ends += ring(r, dense, came[1], came[2])
    return call(functools.partial(finish_kernel, RINGS), jax.ShapeDtypeStruct((VB * BLK, BLK), jnp.float32), ends, 0)


def solution(mesh):
    placed = (
        P("dev", "grp"),
        P(),
        P("grp", "dev", None, None),
        P("grp", "dev", None, None),
        P("grp", "dev", None),
        P("grp", "dev", None, None, None, None),
    )

    return jax.shard_map(body, mesh=mesh, in_specs=placed, out_specs=P(("grp", "dev"), None), check_vma=False)
```

```python
import functools

import jax
import jax.numpy as jnp
from jax import lax
from jax.experimental import pallas as pl
from jax.experimental.pallas import tpu as pltpu
from jax.sharding import PartitionSpec as P


BLK = 128
CAP = 16
CORES = 2
NX = 4
NY = 4
NZ = 8
VB = 16
PART = CORES * CAP
CHUNKS = (32, 48, 48)
HOPS = NZ // 2
VMEM_LIMIT = 10 << 20
RINGS = ((1,), (2,))
FOLDS = (0,)
BITS = 3


VMEM = pl.BlockSpec(memory_space=pltpu.VMEM)
SMEM = pl.BlockSpec(memory_space=pltpu.SMEM)


def call(kernel, out_shape, ins, smems, flops=0, scratch=(), aliases=None):
    specs = [SMEM] * smems + [VMEM] * (len(ins) - smems)
    many = isinstance(out_shape, list)
    return pl.pallas_call(
        kernel,
        out_shape=out_shape,
        in_specs=specs,
        out_specs=[VMEM] * len(out_shape) if many else VMEM,
        scratch_shapes=list(scratch),
        input_output_aliases=aliases or {},
        compiler_params=pltpu.CompilerParams(vmem_limit_bytes=VMEM_LIMIT),
        cost_estimate=pl.CostEstimate(flops=flops, bytes_accessed=4 << 20, transcendentals=0),
    )(*ins)


def adjoint_kernel(rows, sides, begun, rays_ref, place_ref, *refs):
    given, outs = refs[: 2 * len(sides)], refs[2 * len(sides) + begun :]
    low, high = rows[0][0], rows[-1][1]
    size = high - low
    blank = jnp.zeros((size, BLK), jnp.bfloat16)
    for k in range(NX):
        to = lax.rem(place_ref[0] + k, NX)
        for side, proj, tiles in zip(sides, given[::2], given[1::2]):

            for quad in range(CAP // 4):
                first = (k * CORES + side) * CAP + quad * 4
                stack = []
                for v in range(4):
                    ray = rays_ref[first + v]
                    rank = proj[low:high, pl.ds(pl.multiple_of(jnp.maximum(ray, 0) * BLK, BLK), BLK)]
                    rank = jnp.where(ray >= 0, rank, blank)
                    stack.append(jnp.concatenate([blank, rank] if v % 2 else [rank, blank], axis=1))
                made = jnp.dot(
                    jnp.concatenate(stack, axis=0),
                    jnp.concatenate([tiles[to, quad * 2], tiles[to, quad * 2 + 1]], axis=1),
                    preferred_element_type=jnp.float32,
                )
                for v in range(4):
                    block = made[v * size : (v + 1) * size, (v // 2) * BLK : (v // 2 + 1) * BLK].astype(jnp.bfloat16)
                    for j, (lo, hi) in enumerate(rows):
                        outs[j * NX + k][side * CAP + quad * 4 + v] = block[lo - low : hi - low]


def pack_kernel(src_ref, *refs):
    ins, outs, buf = refs[:NX], refs[NX : NX + NY], refs[NX + NY]
    for k in range(NX):
        buf[k * PART : (k + 1) * PART] = ins[k][...]
    for k in range(NY):

        def move(i, carry, k=k):
            for u in range(8):
                p = i * 8 + u
                outs[k][p] = buf[src_ref[k * PART + p]]
            return carry

        lax.fori_loop(0, PART // 8, move, 0)


def gather_kernel(fars, earlier, at_ref, *refs):
    ins, before, dense = refs[:NY], refs[NY : NY + earlier], refs[NY + earlier]
    sends = refs[NY + earlier + 1 :]
    dense[...] = jnp.zeros_like(dense)
    for k in range(NY):

        def add(i, carry, k=k):
            for u in range(4):
                p = i * 4 + u
                at = at_ref[k * PART + p]
                dense[at] = dense[at] + ins[k][p].astype(jnp.float32)
            return carry

        lax.fori_loop(0, PART // 4, add, 0)
    for send, far in zip(sends, fars):
        low = 0
        for part in tuple(before) + (dense,):
            high = low + part.shape[1]
            send[:, low:high, :] = part[far * VB : far * VB + send.shape[0]].astype(jnp.bfloat16)
            low = high


def hop_kernel(places, count, *refs):
    dense, refs = refs[:count], refs[count:]
    n = len(places)
    for came, goes, at in zip(refs[:n], refs[n:], places):
        low = 0
        for part in dense:
            high = low + part.shape[1]
            mine = part[at * VB : (at + 1) * VB]
            goes[:, low:high, :] = (came[:, low:high, :].astype(jnp.float32) + mine).astype(jnp.bfloat16)
            low = high


def fold_kernel(keep, came, goes, kept):
    half = kept.shape[0]
    kept[...] = keep[:half] + came[:half].astype(jnp.float32)
    goes[...] = (keep[half : 2 * half] + came[half:].astype(jnp.float32)).astype(jnp.bfloat16)


def finish_kernel(folds, groups, *refs):
    parts, out = refs[:-1], refs[-1]
    for b in range(VB):
        rows = []
        for i in range(folds):
            rows.append(parts[2 * i][b] + parts[2 * i + 1][b].astype(jnp.float32))
        at = 2 * folds
        for group in groups:
            up, down = parts[at + len(group)], parts[at + len(group) + 1]
            low = 0
            for part in parts[at : at + len(group)]:
                high = low + part.shape[1]
                rows.append(
                    part[b] + up[b, low:high, :].astype(jnp.float32) + down[b, low:high, :].astype(jnp.float32)
                )
                low = high
            at += len(group) + 2
        out[b * BLK : (b + 1) * BLK, :] = jnp.concatenate(rows, axis=0).T


def x_shift(k):
    return [(x * CORES + c, (x + k) % NX * CORES + c) for x in range(NX) for c in range(CORES)]


def core_swap():
    return [(g, g ^ 1) for g in range(NX * CORES)]


def y_shift(k):
    return [(y * NZ + z, (y + k) % NY * NZ + z) for y in range(NY) for z in range(NZ)]


def z_shift(k):
    return [(y * NZ + z, y * NZ + (z + k) % NZ) for y in range(NY) for z in range(NZ)]


def z_fold(step):
    size = NX * CORES * NY * NZ
    pairs = []
    for i in range(size):
        g, d = divmod(i, NY * NZ)
        z, c = d % NZ, g % CORES
        pairs.append((i, i - z + (((z + c) % NZ ^ (1 << step)) - c) % NZ))
    return pairs


def exchange(parts, axis, shift):
    moved = [parts[0]]
    for k in range(1, len(parts)):
        moved.append(lax.ppermute(parts[k], axis, shift(k)))
    return moved


def spread(known, axis, near):
    for pairs in near:
        known = jnp.concatenate([known, lax.ppermute(known, axis, pairs)], axis=0)
    return known


def flip(size, unit, bit):
    return [(i, i ^ (bit * unit)) for i in range(size)]


def turned(e):
    return (e & 1) * 4 + (e & 2) + e // 4


def routes(slot_ray, slot_vox, slot_count, x, c, y, z):
    used = jnp.arange(CAP, dtype=jnp.int32)[None, :] < slot_count[:, None]
    lists = jnp.concatenate([jnp.where(used, slot_ray, -1), slot_vox], axis=1)
    size = NX * CORES
    near = [flip(size, 1, 1), flip(size, CORES, 1), flip(size, CORES, 2)]
    table = spread(lists[None], "grp", near)
    table = table.reshape(NX, CORES, NX, CORES, 2 * CAP)
    mine = lax.dynamic_index_in_dim(table, c, 3, keepdims=False)
    rays = lax.dynamic_slice_in_dim(jnp.concatenate([mine[0]] * 2, axis=1), x, NX, 1)
    rays = jnp.transpose(rays, (1, 0, 2))[:, :, :CAP].reshape(NX * PART)
    vox = lax.dynamic_index_in_dim(mine, x, 2, keepdims=False)[:, :, CAP:].reshape(NX, PART)
    entry = jnp.bitwise_xor(x, lax.rem(x - jnp.arange(NX, dtype=jnp.int32) + NX, NX))
    pick = (entry[:, None] == jnp.arange(NX, dtype=jnp.int32)[None, :]).astype(jnp.int32)
    vox = jnp.sum(pick[:, :, None] * vox[None], axis=1).reshape(1, NX * PART)
    near = [flip(NY * NZ, NZ, 1), flip(NY * NZ, NZ, 2)]
    vox = spread(vox, "dev", near)
    key = lax.rem(vox // (NZ * VB), NY)
    there = jnp.bitwise_xor(y, jnp.arange(NY, dtype=jnp.int32))
    turn = lax.rem(key - there[:, None] + NY, NY)
    slots = jnp.arange(NX * PART, dtype=jnp.int32)
    same = (turn[:, :, None] == turn[:, None, :]) & (slots[None, None, :] < slots[None, :, None])
    target = turn * PART + jnp.sum(same.astype(jnp.int32), axis=2)
    hit = (target[:, None, :] == slots[None, :, None]).astype(jnp.int32)
    src = jnp.sum(hit[0] * slots[None, :], axis=1)
    near_z = lax.rem(lax.rem(vox // VB, NZ) - z + NZ, NZ)
    fold_z = turned(jnp.bitwise_xor(lax.rem(lax.rem(vox // VB, NZ) + c, NZ), lax.rem(z + c, NZ)))
    entry = jnp.bitwise_xor(y, lax.rem(y - jnp.arange(NY, dtype=jnp.int32) + NY, NY))
    pick = (entry[:, None] == jnp.arange(NY, dtype=jnp.int32)[None, :]).astype(jnp.int32)
    both = (near_z * VB + lax.rem(vox, VB)) * (NZ * VB) + fold_z * VB + lax.rem(vox, VB)
    both = jnp.sum(hit * both[:, None, :], axis=2).reshape(NY, NY, PART)
    both = jnp.sum(pick[:, :, None] * jnp.transpose(both, (1, 0, 2)), axis=1).reshape(NY * PART)
    return rays, src, both // (NZ * VB), lax.rem(both, NZ * VB)


def turns(r):
    up_far = HOPS - r % 2
    return list(range(up_far, 0, -1)), list(range(up_far + 1, NZ))


def ways(r):
    return sorted(zip(("up", "down"), turns(r)), key=lambda way: -len(way[1]))


def ring(r, dense, up, down):
    ends = dict(up=up, down=down)
    for way, far in ways(r):
        part = ends[way]
        for hop in range(len(far)):
            part = lax.ppermute(part, "dev", z_shift(1 if way == "up" else NZ - 1))
            if hop + 1 < len(far):
                (part,) = call(
                    functools.partial(hop_kernel, far[hop + 1 : hop + 2], len(dense)),
                    [pltpu.VMEM(part.shape, part.dtype)],
                    dense + [part],
                    0,
                )
        ends[way] = part
    return dense + [ends["up"], ends["down"]]


def body(residual, coefficients, slot_ray, slot_vox, slot_count, footprint):
    g, d = lax.axis_index("grp"), lax.axis_index("dev")
    x, c, y, z = g // CORES, g % CORES, d // NZ, d % NZ
    panel = lax.all_to_all(residual, "dev", split_axis=1, concat_axis=0, tiled=True)
    tables = routes(slot_ray[0, 0], slot_vox[0, 0], slot_count[0, 0], x, c, y, z)
    place = jnp.stack([x, c]).astype(jnp.int32)
    tiles = footprint.reshape(NX, CORES, CAP // 2, 2 * BLK, BLK)
    fpo = lax.dynamic_index_in_dim(tiles, c, 1, keepdims=False)
    fpr = lax.dynamic_index_in_dim(tiles, 1 - c, 1, keepdims=False)
    fpr = lax.ppermute(fpr, "grp", core_swap())
    panel, (rays, src, at, at_fold), place, fpo, fpr = lax.optimization_barrier((panel, tables, place, fpo, fpr))
    own = lax.dot_general(
        coefficients, panel, (((0,), (0,)), ((), ())), preferred_element_type=jnp.float32
    ).astype(jnp.bfloat16)
    par = lax.ppermute(own, "grp", core_swap())
    rows = [(sum(CHUNKS[:i]), sum(CHUNKS[: i + 1])) for i in range(len(CHUNKS))]
    made = []
    for name, some, sides in (("adjo", rows[:1], (0,)), ("adj0", rows[:1], (1,)), ("adj1", rows[1:], (0, 1))):
        begun = made if name == "adj0" else []
        ins = [rays, place]
        for side in sides:
            ins += [(own, par)[side], (fpo, fpr)[side]]
        parts = call(
            functools.partial(adjoint_kernel, some, sides, len(begun)),
            [pltpu.VMEM((PART, hi - lo, BLK), jnp.bfloat16) for lo, hi in some for _ in range(NX)],
            ins + list(begun),
            2,
            aliases={len(ins) + j: j for j in range(len(begun))},
        )
        made = list(parts) if name != "adj1" else made + list(parts)

    def arrive(i):
        block = pltpu.VMEM((PART, CHUNKS[i], BLK), jnp.bfloat16)
        parts = exchange(made[i * NX : (i + 1) * NX], "grp", x_shift)
        parts = call(
            pack_kernel, [block] * NY, [src] + parts, 1, scratch=[pltpu.VMEM((NX * PART, CHUNKS[i], BLK), jnp.bfloat16)]
        )
        return exchange(parts, "dev", y_shift)

    ends = []
    for i in FOLDS:
        parts = arrive(i)
        half = NZ * VB // 2
        tail = (CHUNKS[i], BLK)
        keep, part = call(
            functools.partial(gather_kernel, (NZ // 2,), 0),
            [pltpu.VMEM((NZ * VB,) + tail, jnp.float32), pltpu.VMEM((half,) + tail, jnp.bfloat16)],
            [at_fold] + parts,
            1,
        )
        for step in range(BITS):
            part = lax.ppermute(part, ("grp", "dev"), z_fold(step))
            if step < BITS - 1:
                half //= 2
                part, keep = call(
                    fold_kernel,
                    [pltpu.VMEM((half,) + tail, jnp.bfloat16), pltpu.VMEM((half,) + tail, jnp.float32)],
                    [keep, part],
                    0,
                )
        ends += [keep, part]
    for r, group in enumerate(RINGS):
        dense = []
        for i in group:
            parts = arrive(i)
            sends = []
            if i == group[-1]:
                sends = [pltpu.VMEM((VB, sum(CHUNKS[j] for j in group), BLK), jnp.bfloat16)] * 2
            before = dense if sends else []
            far = turns(r)[0][0]
            came = call(
                functools.partial(gather_kernel, (far, far + 1), len(before)),
                [pltpu.VMEM((NZ * VB, CHUNKS[i], BLK), jnp.float32)] + sends,
                [at] + parts + before,
                1,
            )
            dense = dense + [came[0]]
        ends += ring(r, dense, came[1], came[2])
    return call(
        functools.partial(finish_kernel, len(FOLDS), RINGS), jax.ShapeDtypeStruct((VB * BLK, BLK), jnp.float32), ends, 0
    )


def solution(mesh):
    placed = (
        P("dev", "grp"),
        P(),
        P("grp", "dev", None, None),
        P("grp", "dev", None, None),
        P("grp", "dev", None),
        P("grp", "dev", None, None, None, None),
    )

    return jax.shard_map(body, mesh=mesh, in_specs=placed, out_specs=P(("grp", "dev"), None), check_vma=False)
```
